512 devices in a mesh: band: 32 (over y_hi, z, core), ga: 16 (over y_lo, x).
Axes of the slice: x: 4, y: 8 (y_hi: 2, y_lo: 4; y = y_hi * 4 + y_lo), z: 8, core: 2. Of those that a mesh axis runs over, the one named last changes fastest.
Arguments:
- valence_pairs: bfloat16 [1024, 10240], P(None, 'band'), may hold values from -6 to 6
- screened: bfloat16 [10240, 10240], P('band', 'ga'), may hold values from -0.0625 to 0.0625
- conduction_pairs: bfloat16 [65536, 10240], P('band', 'ga'), may hold values from -0.0625 to 0.0625
- window_mask: int32 [8, 512], P(None, 'band'), may hold values 0 or 1
Outputs:
- direct_kernel: bfloat16 [1024, 65536], P('ga', 'band')
The draws below stay inside these ranges and needn't reach their ends.
All inputs are finite; a program needn't handle non-finite values. No bound on the sum of `window_mask` on one device may be relied on, other than what follows from the above.
Results may differ from the reference program's by a relative error of at most 0.017.
Values may be sent and summed in bfloat16 or wider, within the bound.
A program may use at most 64 MiB of HBM per device.

```python
import jax
import jax.numpy as jnp
from jax import lax

NG = 10240
BLOCK = 128
VP = 1024
CP = 65536
N_GA = 16


def plant(result, key, least, high):
    extent = result.shape
    place = [jax.random.randint(jax.random.fold_in(key, axis), (), 0, extent[axis]) for axis in range(len(extent))]
    result = result.at[tuple(place)].set(least)
    longest = extent.index(max(extent))
    place[longest] = (place[longest] + 1) % extent[longest]
    return result.at[tuple(place)].set(high)


def levels(own_key, extent, cuts, low, high):
    factor_of = 1.0
    for position, shards_of in cuts:
        heights = jax.random.uniform(jax.random.fold_in(jax.random.fold_in(own_key, 6), position), (shards_of,), jnp.float32, low / len(cuts), high / len(cuts))
        factor_of = factor_of * jnp.repeat(jnp.exp(heights), extent[position] // shards_of).reshape((-1,) + (1,) * (len(extent) - 1 - position))
    return factor_of


def scatter_about(key, shape, deviation, reach, shards=(), kind=jnp.bfloat16):
    gain = levels(key, shape, shards, -0.22, 0.18) if shards else 1.0
    drawn = jax.random.normal(key, shape, jnp.float32) * deviation * gain
    return jnp.minimum(jnp.maximum(drawn, -reach), reach).astype(kind)


def setup_inputs(seed: int = 0) -> dict:
    streams_of = jax.random.split(jax.random.key(seed), 5)
    valence_pairs = scatter_about(streams_of[0], (VP, NG), 1.0, 6.0, ((1, 32),))
    screened = scatter_about(streams_of[1], (NG, NG), NG ** -0.5, 0.0625, ((0, 32), (1, 16)))
    conduction_pairs = scatter_about(streams_of[2], (CP, NG), NG ** -0.5, 0.0625, ((0, 32), (1, 16)))
    window_mask = plant((jax.random.randint(streams_of[3], (VP // BLOCK, CP // BLOCK), 0, 3) < 2).astype(jnp.int32), jax.random.fold_in(streams_of[3], 1), 0, 1)
    return dict(valence_pairs=valence_pairs, screened=screened, conduction_pairs=conduction_pairs, window_mask=window_mask)


def reference(valence_pairs, screened, conduction_pairs, window_mask):
    screened_valence = jnp.dot(valence_pairs, screened, preferred_element_type=jnp.float32).astype(jnp.bfloat16)
    width = NG // N_GA
    total = jnp.zeros((VP, CP), jnp.float32)
    for shard in range(N_GA):
        left = screened_valence[:, shard * width:(shard + 1) * width]
        right = conduction_pairs[:, shard * width:(shard + 1) * width]
        partial_value = lax.dot_general(left, right, (((1,), (1,)), ((), ())), preferred_element_type=jnp.float32)
        rounded = lax.optimization_barrier(partial_value.astype(jnp.bfloat16))
        total = total + rounded.astype(jnp.float32)
    live = jnp.repeat(jnp.repeat(window_mask, BLOCK, axis=0), BLOCK, axis=1).astype(jnp.float32)
    return (total * live).astype(jnp.bfloat16)
```

```python
import jax
import jax.numpy as jnp
from jax import lax
from jax.experimental import pallas as pl
from jax.experimental.pallas import tpu as pltpu
from jax.sharding import Mesh
from jax.sharding import PartitionSpec as P

MESH = pl.DeviceIdType.MESH
BAND = ("yh", "z", "c")
GA = ("y", "x")
F32 = jnp.float32
BF16 = jnp.bfloat16

NZ, NY, NX = 8, 4, 4
NJ = 4
RW = 16
SPLIT = 1536
HOPS = (4, 3, 5, 2, 6, 1, 7)


def schedule():
    start = (0.0, 3.0, 13.0, 20.0)
    first = 25.0
    events = []
    for j in range(NJ):
        t = start[j]
        for name, dt in (("S0", 0), ("S1", 2.5), ("S2", 10), ("S3", 15), ("S4", 23)):
            events.append((t + dt, name, j))
        t = first + 7.4 * j
        for name, dt in (
            ("PB", 0), ("BY0", 0.1), ("PA", 0.2), ("AX1", 0.3),
            ("AX2", 5), ("BY1", 5.1), ("AX3", 9), ("AY0", 9.1), ("BY2", 9.2),
            ("AY1", 13), ("BY3", 13.1), ("BX1", 13.2), ("AY2", 16), ("BX2", 16.1),
            ("AY3", 19), ("AF", 19.1), ("BX3", 19.2),
        ):
            events.append((t + dt, name, j))
    events.sort(key=lambda e: e[0])
    return [(name, j) for _, name, j in events]


def kernel(v_hbm, w_hbm, c_hbm, mask, out, v, w, cc, core_s, core_r, own, zs, zr, ysum, ys, yr,
           sv, pb, rb, rb16, ra, xra, xsa, xrb, xsb, yra, ysa, yrb, ysb,
           in_sem, one_s, one_r, xa_s, xa_r, xb_s, xb_r, y_s, y_r):
    yh, z, c = lax.axis_index("yh"), lax.axis_index("z"), lax.axis_index("c")
    y, x = lax.axis_index("y"), lax.axis_index("x")
    xp, xf, xm = lax.rem(x + 1, NX), lax.rem(x + 2, NX), lax.rem(x + 3, NX)

    loads = [
        pltpu.make_async_copy(v_hbm, v, in_sem.at[0]),
        pltpu.make_async_copy(w_hbm, w, in_sem.at[1]),
        pltpu.make_async_copy(c_hbm, cc, in_sem.at[2]),
    ]
    for load in loads:
        load.start()

    def at_z(k):
        return (yh, lax.rem(z + k, NZ), c, y, x)

    partner = (yh, z, 1 - c, y, x)
    far = (1 - yh, z, c, y, x)
    right, left = (yh, z, c, y, xp), (yh, z, c, y, xm)
    up, down = (yh, z, c, y + 1, x), (yh, z, c, y - 1, x)

    barrier = pltpu.get_barrier_semaphore()

    def greet(device):
        pl.semaphore_signal(barrier, inc=1, device_id=device, device_id_type=MESH)

    for k in HOPS:
        greet(at_z(k))
    for device in (far, right, left, partner):
        greet(device)
    pl.when(y < NY - 1)(lambda: greet(up))
    pl.when(y > 0)(lambda: greet(down))

    def send(src, dst, s_sem, r_sem, device):
        pltpu.make_async_remote_copy(
            src_ref=src, dst_ref=dst, send_sem=s_sem, recv_sem=r_sem,
            device_id=device, device_id_type=MESH,
        ).start()

    def arrived(ref, sem):
        pltpu.make_async_copy(ref, ref, sem).wait()

    def partial(half, j):
        rows = v[pl.ds(half * 8, 8), j * RW:(j + 1) * RW, :].reshape(128, -1)
        return jnp.dot(rows, w[...], preferred_element_type=F32).reshape(8, RW, -1)

    def S0(j):
        core_s[j] = partial(1 - c, j).astype(BF16)
        if j == 0:
            pl.semaphore_wait(
                barrier, 11 + (y > 0).astype(jnp.int32) + (y < NY - 1).astype(jnp.int32)
            )
        send(core_s.at[j], core_r.at[j], one_s.at[j, 0], one_r.at[j, 0], partner)
        own[j] = partial(c, j)

    def S1(j):
        arrived(core_r.at[j], one_r.at[j, 0])
        total = own[j] + core_r[j].astype(F32)
        own[j] = total
        zs[j] = total.astype(BF16)
        for k in HOPS:
            send(zs.at[j, lax.rem(z + k, NZ)], zr.at[j, k - 1],
                 one_s.at[j, 1], one_r.at[j, 1], at_z(k))

    def S2(j):
        arrived(zr.at[j], one_r.at[j, 1])
        total = own[j, z]
        for k in range(NZ - 1):
            total = total + zr[j, k].astype(F32)
        ysum[j] = total
        ys[j] = total.astype(BF16)
        send(ys.at[j], yr.at[j], one_s.at[j, 2], one_r.at[j, 2], far)

    def S3(j):
        arrived(yr.at[j], one_r.at[j, 2])
        mine = c * NZ + z
        sv[j, mine] = (ysum[j] + yr[j].astype(F32)).astype(BF16)
        for k in HOPS:
            send(sv.at[j, mine], sv.at[j, mine], one_s.at[j, 3], one_r.at[j, 3], at_z(k))

    def S4(j):
        arrived(zr.at[j], one_r.at[j, 3])
        half = sv.at[j, pl.ds(c * NZ, NZ)]
        send(half, half, one_s.at[j, 4], one_r.at[j, 4], partner)

    def product(j, first, count):
        rows = sv[j].reshape(256, -1)

        def tile(t, carry):
            at = pl.multiple_of(first + t * 256, 256)
            block = lax.dot_general(
                rows, cc[pl.ds(at, 256), :], (((1,), (1,)), ((), ())), preferred_element_type=F32
            )
            pb[j, :, :, :, pl.ds(at, 256)] = block.astype(BF16).reshape(NY, NX, RW, 256)
            return carry

        lax.fori_loop(0, count // 256, tile, 0)

    width = out.shape[1]
    tail = width - SPLIT
    b_cols = pl.ds(SPLIT, tail)

    def PB(j):
        arrived(sv.at[j, pl.ds(0, NZ)], one_r.at[j, 4])
        if j == 0:
            loads[2].wait()
        product(j, SPLIT, tail)

    def PA(j):
        product(j, 0, SPLIT)

    half_a, half_b = SPLIT // 2, tail // 2

    def a_part(j, i, half):
        return pb.at[j, :, i, :, pl.ds(half * half_a, half_a)]

    def b_part(j, i, half):
        return rb16.at[j, i, :, pl.ds(half * half_b, half_b)]

    def x_first(j, part, got, s_sem, r_sem):
        send(part(j, xf, 0), got.at[j, 0], s_sem.at[j, 0], r_sem.at[j, 0], right)
        send(part(j, xf, 1), got.at[j, 3], s_sem.at[j, 3], r_sem.at[j, 3], left)
        send(part(j, xp, 1), got.at[j, 1], s_sem.at[j, 1], r_sem.at[j, 1], right)
        send(part(j, xm, 0), got.at[j, 4], s_sem.at[j, 4], r_sem.at[j, 4], left)

    def x_second(j, part, got, out_buf, s_sem, r_sem):
        for slot, i, half, device in ((0, xp, 0, right), (3, xm, 1, left)):
            arrived(got.at[j, slot], r_sem.at[j, slot])
            mine = part(j, i, half)[...]
            out_buf[j, slot // 3] = (mine.astype(F32) + got[j, slot].astype(F32)).astype(BF16)
            send(out_buf.at[j, slot // 3], got.at[j, slot + 2],
                 s_sem.at[j, slot + 2], r_sem.at[j, slot + 2], device)

    def x_third(j, got, r_sem, half):
        a, b = ((2, 4), (1, 5))[half]
        arrived(got.at[j, a], r_sem.at[j, a])
        arrived(got.at[j, b], r_sem.at[j, b])
        return got[j, a].astype(F32) + got[j, b].astype(F32)

    def AX1(j):
        x_first(j, a_part, xra, xa_s, xa_r)

    def AX2(j):
        x_second(j, a_part, xra, xsa, xa_s, xa_r)

    def AX3(j):
        for half in (0, 1):
            ra[j, :, :, half * half_a:(half + 1) * half_a] = (
                x_third(j, xra, xa_r, half) + a_part(j, x, half)[...].astype(F32)
            )

    def BX1(j):
        rb16[j] = rb[j].astype(BF16)
        x_first(j, b_part, xrb, xb_s, xb_r)

    def BX2(j):
        x_second(j, b_part, xrb, xsb, xb_s, xb_r)

    row_block = (y * NX + x) // 2

    def finish(j, first, value):
        for t in range(value.shape[1] // 128):
            live = mask[row_block, first // 128 + t].astype(F32)
            out[j * RW:(j + 1) * RW, first + t * 128:first + (t + 1) * 128] = (
                value[:, t * 128:(t + 1) * 128] * live
            ).astype(BF16)

    def BX3(j):
        for half in (0, 1):
            value = x_third(j, xrb, xb_r, half) + rb[j, x, :, half * half_b:(half + 1) * half_b]
            finish(j, SPLIT + half * half_b, value)

    def AF(j):
        finish(j, 0, ra[j, y])

    def y_step(j, h, p):
        got, buf = (yra, ysa) if p == 0 else (yrb, ysb)

        def own_blocks(lo, hi):
            if p == 0:
                return ra[j, lo:hi]
            return pb[j, lo:hi, :, :, SPLIT:].astype(F32)

        def one_way(d):
            lo, hi = (h + 1, NY) if d == 0 else (0, NY - 1 - h)
            keep = h if d == 0 else NY - 1 - h
            if h > 0:
                block = got.at[j, d, keep:NY] if d == 0 else got.at[j, d, 0:keep + 1]
                arrived(block, y_r.at[j, p, d])
                if p == 0:
                    ra[j, keep] = ra[j, keep] + got[j, d, keep].astype(F32)
                else:
                    rb[j] = rb[j] + got[j, d, keep].astype(F32)
            if h < NY - 1:
                if p == 1 and h == 0:
                    src = pb.at[j, lo:hi, :, :, b_cols]
                else:
                    value = own_blocks(lo, hi)
                    if h > 0:
                        value = value + got[j, d, lo:hi].astype(F32)
                    buf[j, d, lo:hi] = value.astype(BF16)
                    src = buf.at[j, d, lo:hi]
                send(src, got.at[j, d, lo:hi], y_s.at[j, p], y_r.at[j, p, d], up if d == 0 else down)

        if p == 1 and h == 0:
            rb[j] = pb[j, y, :, :, SPLIT:].astype(F32)
        pl.when(y == h)(lambda: one_way(0))
        pl.when(y == NY - 1 - h)(lambda: one_way(1))

    steps = dict(S0=S0, S1=S1, S2=S2, S3=S3, S4=S4, PB=PB, PA=PA, AX1=AX1, AX2=AX2, AX3=AX3,
                 BX1=BX1, BX2=BX2, BX3=BX3, AF=AF)
    for h in range(NY):
        steps[f"AY{h}"] = lambda j, h=h: y_step(j, h, 0)
        steps[f"BY{h}"] = lambda j, h=h: y_step(j, h, 1)

    loads[0].wait()
    loads[1].wait()
    for name, j in schedule():
        steps[name](j)

    for j in range(NJ):
        arrived(core_s.at[j], one_s.at[j, 0])
        arrived(zr.at[j], one_s.at[j, 1])
        arrived(ys.at[j], one_s.at[j, 2])
        arrived(zr.at[j], one_s.at[j, 3])
        arrived(sv.at[j, pl.ds(0, NZ)], one_s.at[j, 4])
        for slot in range(6):
            arrived(xra.at[j, slot], xa_s.at[j, slot])
            arrived(xrb.at[j, slot], xb_s.at[j, slot])
        arrived(yra.at[j, 0, 0:3], y_s.at[j, 0])
        arrived(yrb.at[j, 0, 0:3], y_s.at[j, 1])


def local(valence_pairs, screened, conduction_pairs, window_mask):
    rows, depth = valence_pairs.shape
    inner = screened.shape[1]
    width = conduction_pairs.shape[0]
    tail = width - SPLIT
    v3 = valence_pairs.reshape(NY * NX, rows // (NY * NX), depth)
    vmem, dma = pltpu.VMEM, pltpu.SemaphoreType.DMA
    any_space = pl.BlockSpec(memory_space=pl.ANY)
    scratch = [
        vmem(v3.shape, BF16), vmem(screened.shape, BF16), vmem(conduction_pairs.shape, BF16),
        vmem((NJ, NZ, RW, inner), BF16), vmem((NJ, NZ, RW, inner), BF16),
        vmem((NJ, NZ, RW, inner), F32),
        vmem((NJ, NZ, RW, inner), BF16), vmem((NJ, NZ - 1, RW, inner), BF16),
        vmem((NJ, RW, inner), F32), vmem((NJ, RW, inner), BF16), vmem((NJ, RW, inner), BF16),
        vmem((NJ, 2 * NZ, RW, inner), BF16),
        vmem((NJ, NY, NX, RW, width), BF16),
        vmem((NJ, NX, RW, tail), F32), vmem((NJ, NX, RW, tail), BF16),
        vmem((NJ, NY, RW, SPLIT), F32),
        vmem((NJ, 6, NY, RW, SPLIT // 2), BF16), vmem((NJ, 2, NY, RW, SPLIT // 2), BF16),
        vmem((NJ, 6, RW, tail // 2), BF16), vmem((NJ, 2, RW, tail // 2), BF16),
        vmem((NJ, 2, NY, RW, SPLIT), BF16), vmem((NJ, 2, NY, RW, SPLIT), BF16),
        vmem((NJ, 2, NY, NX, RW, tail), BF16), vmem((NJ, 2, NY, NX, RW, tail), BF16),
        dma((3,)), dma((NJ, 5)), dma((NJ, 5)),
        dma((NJ, 6)), dma((NJ, 6)), dma((NJ, 6)), dma((NJ, 6)),
        dma((NJ, 2)), dma((NJ, 2, 2)),
    ]
    return pl.pallas_call(
        kernel,
        out_shape=jax.ShapeDtypeStruct((rows // (NY * NX), width), BF16),
        in_specs=[any_space, any_space, any_space, pl.BlockSpec(memory_space=pltpu.SMEM)],
        out_specs=pl.BlockSpec(memory_space=pltpu.VMEM),
        scratch_shapes=scratch,
        compiler_params=pltpu.CompilerParams(
            collective_id=0, has_side_effects=True, vmem_limit_bytes=56 * 1024 * 1024
        ),
        name="window",
    )(v3, screened, conduction_pairs, window_mask)


def solution(mesh):
    torus = Mesh(mesh.devices.reshape(2, NZ, 2, NY, NX), BAND + GA)
    return jax.shard_map(
        local,
        mesh=torus,
        in_specs=(P(None, BAND), P(BAND, GA), P(BAND, GA), P(None, BAND)),
        out_specs=P(GA, BAND),
        check_vma=False,
    )
```

```python
import jax
import jax.numpy as jnp
from jax import lax
from jax.experimental import pallas as pl
from jax.experimental.pallas import tpu as pltpu
from jax.sharding import Mesh
from jax.sharding import PartitionSpec as P

MESH = pl.DeviceIdType.MESH
BAND = ("yh", "z", "c")
GA = ("y", "x")
F32 = jnp.float32
BF16 = jnp.bfloat16

NZ, NY, NX = 8, 4, 4
NJ = 4
RW = 16
SPLIT = 1792
HOPS = (4, 3, 5, 2, 6, 1, 7)
UNITS = (((0, 1024), (1024, 768)),) * NJ


def schedule():
    times = {
        "S1": (2.5, 2.6, 11.1, 20.2), "S2": (11, 15.3, 20.3, 30),
        "S3": (15.8, 20.1, 25.2, 35), "S4": (21.7, 26.5, 31.5, 41),
    }
    events = [(t, name, j, 0) for name, row in times.items() for j, t in enumerate(row)]
    for j in range(NJ):
        t = 23 + 7.7 * j
        for dt, name, u in (
            (0, "PB", 0), (0.1, "XF", 0), (0.2, "XD", 0), (0.3, "XF", 1),
            (5.0, "X2", 0), (5.1, "XD", 1), (7.2, "X2", 1), (7.3, "BS", 0), (9.5, "X3", 0), (12, "X3", 1),
            (12.1, "B2", 0), (16, "B3", 0), (17, "YF", 0), (19, "YF", 1),
        ):
            events.append((t + dt, name, j, u))
    events.sort(key=lambda e: e[0])
    return [e[1:] for e in events]


def kernel(v_hbm, w_hbm, c_hbm, mask, out, v, w, cc, core_s, core_r, own, zs, zr, ysum, ys, yr,
           sv, pb, far_r, dir_r, mrg_s, mrg_r, ya_s, ya_r, yb_r, rb, rb16, bfar, bdir, bms, bmr,
           in_sem, one_s, one_r, xa_s, xa_r, ya_ss, ya_rs, yb_ss, yb_rs, xb_s, xb_r):
    yh, z, c = lax.axis_index("yh"), lax.axis_index("z"), lax.axis_index("c")
    y, x = lax.axis_index("y"), lax.axis_index("x")
    xp, xf, xm = lax.rem(x + 1, NX), lax.rem(x + 2, NX), lax.rem(x + 3, NX)

    loads = [
        pltpu.make_async_copy(v_hbm, v, in_sem.at[0]),
        pltpu.make_async_copy(w_hbm, w, in_sem.at[1]),
        pltpu.make_async_copy(c_hbm, cc, in_sem.at[2]),
    ]
    loads[0].start()
    loads[1].start()

    def at_z(k):
        return (yh, lax.rem(z + k, NZ), c, y, x)

    def at_y(k):
        return (yh, z, c, lax.rem(y + k, NY), x)

    partner = (yh, z, 1 - c, y, x)
    far = (1 - yh, z, c, y, x)
    right, left = (yh, z, c, y, xp), (yh, z, c, y, xm)

    barrier = pltpu.get_barrier_semaphore()
    peers = [at_z(k) for k in HOPS] + [far] + [at_y(k) for k in (1, 2, 3)] + [right, left, partner]
    for device in peers:
        pl.semaphore_signal(barrier, inc=1, device_id=device, device_id_type=MESH)

    def send(src, dst, s_sem, r_sem, device):
        pltpu.make_async_remote_copy(
            src_ref=src, dst_ref=dst, send_sem=s_sem, recv_sem=r_sem,
            device_id=device, device_id_type=MESH,
        ).start()

    def arrived(ref, sem):
        pltpu.make_async_copy(ref, ref, sem).wait()

    def partial(half, t):
        lanes = pl.ds(pl.multiple_of(half * 512 + t * 128, 128), 128)
        value = lax.dot_general(
            v[:, lanes], w[...], (((0,), (0,)), ((), ())), preferred_element_type=F32
        )
        return value.reshape(2, NJ, RW, -1)

    loads[0].wait()
    loads[1].wait()
    loads[2].start()

    def for_partner(t, carry):
        value = partial(1 - c, t).astype(BF16)
        for j in range(NJ):
            core_s[j, pl.ds(2 * t, 2)] = value[:, j]
        return carry

    lax.fori_loop(0, 4, for_partner, 0)
    pl.semaphore_wait(barrier, len(peers))
    for j in range(NJ):
        send(core_s.at[j], core_r.at[j], one_s.at[j, 0], one_r.at[j, 0], partner)

    def for_self(t, carry):
        value = partial(c, t)
        for j in range(NJ):
            own[j, pl.ds(2 * t, 2)] = value[:, j]
        return carry

    lax.fori_loop(0, 4, for_self, 0)

    def S1(j, u):
        arrived(core_r.at[j], one_r.at[j, 0])
        total = own[j] + core_r[j].astype(F32)
        own[j] = total
        zs[j] = total.astype(BF16)
        for k in HOPS:
            send(zs.at[j, lax.rem(z + k, NZ)], zr.at[j, k - 1],
                 one_s.at[j, 1], one_r.at[j, 1], at_z(k))

    def S2(j, u):
        arrived(zr.at[j], one_r.at[j, 1])
        total = own[j, z]
        for k in range(NZ - 1):
            total = total + zr[j, k].astype(F32)
        ysum[j] = total
        ys[j] = total.astype(BF16)
        send(ys.at[j], yr.at[j], one_s.at[j, 2], one_r.at[j, 2], far)

    def S3(j, u):
        arrived(yr.at[j], one_r.at[j, 2])
        mine = c * NZ + z
        sv[j, mine] = (ysum[j] + yr[j].astype(F32)).astype(BF16)
        for k in HOPS:
            send(sv.at[j, mine], sv.at[j, mine], one_s.at[j, 3], one_r.at[j, 3], at_z(k))

    def S4(j, u):
        arrived(zr.at[j], one_r.at[j, 3])
        half = sv.at[j, pl.ds(c * NZ, NZ)]
        send(half, half, one_s.at[j, 4], one_r.at[j, 4], partner)

    def product(j, first, count):
        rows = sv[j].reshape(256, -1)

        def tile(t, carry):
            at = pl.multiple_of(first + t * 256, 256)
            block = lax.dot_general(
                rows, cc[pl.ds(at, 256), :], (((1,), (1,)), ((), ())), preferred_element_type=F32
            )
            pb[j, :, :, :, pl.ds(at, 256)] = block.astype(BF16).reshape(NY, NX, RW, 256)
            return carry

        lax.fori_loop(0, count // 256, tile, 0)

    width = out.shape[1]
    tail = width - SPLIT
    b_cols = pl.ds(SPLIT, tail)

    def PB(j, u):
        arrived(sv.at[j, pl.ds(0, NZ)], one_r.at[j, 4])
        if j == 0:
            loads[2].wait()
        product(j, SPLIT, tail)
        for k in (3, 2, 1):
            send(pb.at[j, lax.rem(y + k, NY), :, :, b_cols], yb_r.at[j, k - 1],
                 yb_ss.at[j], yb_rs.at[j], at_y(k))

    def halves(j, u):
        lo, w_u = UNITS[j][u]
        return pl.ds(lo, w_u // 2), pl.ds(lo + w_u // 2, w_u // 2)

    def XF(j, u):
        product(j, *UNITS[j][u])
        h0, h1 = halves(j, u)
        send(pb.at[j, :, xf, :, h0], far_r.at[j, :, :, h0], xa_s.at[j, u, 0], xa_r.at[j, u, 0], right)
        send(pb.at[j, :, xf, :, h1], far_r.at[j, :, :, h1], xa_s.at[j, u, 1], xa_r.at[j, u, 1], left)

    def XD(j, u):
        h0, h1 = halves(j, u)
        send(pb.at[j, :, xp, :, h1], dir_r.at[j, :, :, h1], xa_s.at[j, u, 2], xa_r.at[j, u, 2], right)
        send(pb.at[j, :, xm, :, h0], dir_r.at[j, :, :, h0], xa_s.at[j, u, 3], xa_r.at[j, u, 3], left)

    def X2(j, u):
        for i, (h, to, device) in enumerate(zip(halves(j, u), (xp, xm), (right, left))):
            arrived(far_r.at[j, :, :, h], xa_r.at[j, u, i])
            mrg_s[j, :, :, h] = (pb[j, :, to, :, h].astype(F32) + far_r[j, :, :, h].astype(F32)).astype(BF16)
            send(mrg_s.at[j, :, :, h], mrg_r.at[j, :, :, h], xa_s.at[j, u, 4 + i], xa_r.at[j, u, 4 + i], device)

    def X3(j, u):
        h0, h1 = halves(j, u)
        arrived(dir_r.at[j, :, :, h1], xa_r.at[j, u, 2])
        arrived(dir_r.at[j, :, :, h0], xa_r.at[j, u, 3])
        arrived(mrg_r.at[j, :, :, h0], xa_r.at[j, u, 4])
        arrived(mrg_r.at[j, :, :, h1], xa_r.at[j, u, 5])
        cols = pl.ds(*UNITS[j][u])
        for k in (3, 2, 1):
            yd = lax.rem(y + k, NY)
            ya_s[j, k - 1, :, cols] = (
                pb[j, yd, x, :, cols].astype(F32) + dir_r[j, yd, :, cols].astype(F32)
                + mrg_r[j, yd, :, cols].astype(F32)
            ).astype(BF16)
            send(ya_s.at[j, k - 1, :, cols], ya_r.at[j, k - 1, :, cols],
                 ya_ss.at[j, u], ya_rs.at[j, u], at_y(k))

    row_block = (y * NX + x) // 2

    def finish(j, first, value):
        for t in range(value.shape[1] // 128):
            live = mask[row_block, first // 128 + t].astype(F32)
            out[j * RW:(j + 1) * RW, first + t * 128:first + (t + 1) * 128] = (
                value[:, t * 128:(t + 1) * 128] * live
            ).astype(BF16)

    def YF(j, u):
        lo, w_u = UNITS[j][u]
        cols = pl.ds(lo, w_u)
        arrived(ya_r.at[j, :, :, cols], ya_rs.at[j, u])
        total = (
            pb[j, y, x, :, cols].astype(F32) + dir_r[j, y, :, cols].astype(F32)
            + mrg_r[j, y, :, cols].astype(F32)
        )
        for k in range(3):
            total = total + ya_r[j, k, :, cols].astype(F32)
        finish(j, lo, total)

    b0, b1 = pl.ds(0, tail // 2), pl.ds(tail // 2, tail // 2)

    def BS(j, u):
        arrived(yb_r.at[j], yb_rs.at[j])
        total = pb[j, y, :, :, b_cols].astype(F32)
        for k in range(3):
            total = total + yb_r[j, k].astype(F32)
        rb[j] = total
        rb16[j] = total.astype(BF16)
        send(rb16.at[j, xf, :, b0], bfar.at[j, :, b0], xb_s.at[j, 0], xb_r.at[j, 0], right)
        send(rb16.at[j, xf, :, b1], bfar.at[j, :, b1], xb_s.at[j, 1], xb_r.at[j, 1], left)
        send(rb16.at[j, xp, :, b1], bdir.at[j, :, b1], xb_s.at[j, 2], xb_r.at[j, 2], right)
        send(rb16.at[j, xm, :, b0], bdir.at[j, :, b0], xb_s.at[j, 3], xb_r.at[j, 3], left)

    def B2(j, u):
        for i, (h, to, device) in enumerate(zip((b0, b1), (xp, xm), (right, left))):
            arrived(bfar.at[j, :, h], xb_r.at[j, i])
            bms[j, :, h] = (rb[j, to, :, h] + bfar[j, :, h].astype(F32)).astype(BF16)
            send(bms.at[j, :, h], bmr.at[j, :, h], xb_s.at[j, 4 + i], xb_r.at[j, 4 + i], device)

    def B3(j, u):
        arrived(bdir.at[j, :, b1], xb_r.at[j, 2])
        arrived(bdir.at[j, :, b0], xb_r.at[j, 3])
        arrived(bmr.at[j, :, b0], xb_r.at[j, 4])
        arrived(bmr.at[j, :, b1], xb_r.at[j, 5])
        finish(j, SPLIT, rb[j, x] + bdir[j].astype(F32) + bmr[j].astype(F32))

    steps = dict(S1=S1, S2=S2, S3=S3, S4=S4, PB=PB, XF=XF, XD=XD, X2=X2, X3=X3, YF=YF, BS=BS, B2=B2, B3=B3)
    for name, j, u in schedule():
        steps[name](j, u)

    for j in range(NJ):
        arrived(core_s.at[j], one_s.at[j, 0])
        arrived(zr.at[j], one_s.at[j, 1])
        arrived(ys.at[j], one_s.at[j, 2])
        arrived(zr.at[j], one_s.at[j, 3])
        arrived(sv.at[j, pl.ds(0, NZ)], one_s.at[j, 4])
        for u, (lo, w_u) in enumerate(UNITS[j]):
            for slot in range(6):
                arrived(far_r.at[j, :, :, pl.ds(lo, w_u // 2)], xa_s.at[j, u, slot])
            arrived(ya_r.at[j, :, :, pl.ds(lo, w_u)], ya_ss.at[j, u])
        arrived(yb_r.at[j], yb_ss.at[j])
        for slot in range(6):
            arrived(bfar.at[j, :, b0], xb_s.at[j, slot])


def local(valence_pairs, screened, conduction_pairs, window_mask):
    inner = screened.shape[1]
    width = conduction_pairs.shape[0]
    tail = width - SPLIT
    vt = valence_pairs.T
    vmem, dma = pltpu.VMEM, pltpu.SemaphoreType.DMA
    any_space = pl.BlockSpec(memory_space=pl.ANY)
    nu = max(len(units) for units in UNITS)
    scratch = [
        vmem(vt.shape, BF16), vmem(screened.shape, BF16), vmem(conduction_pairs.shape, BF16),
        vmem((NJ, NZ, RW, inner), BF16), vmem((NJ, NZ, RW, inner), BF16),
        vmem((NJ, NZ, RW, inner), F32),
        vmem((NJ, NZ, RW, inner), BF16), vmem((NJ, NZ - 1, RW, inner), BF16),
        vmem((NJ, RW, inner), F32), vmem((NJ, RW, inner), BF16), vmem((NJ, RW, inner), BF16),
        vmem((NJ, 2 * NZ, RW, inner), BF16),
        vmem((NJ, NY, NX, RW, width), BF16),
        vmem((NJ, NY, RW, SPLIT), BF16), vmem((NJ, NY, RW, SPLIT), BF16),
        vmem((NJ, NY, RW, SPLIT), BF16), vmem((NJ, NY, RW, SPLIT), BF16),
        vmem((NJ, NY - 1, RW, SPLIT), BF16), vmem((NJ, NY - 1, RW, SPLIT), BF16),
        vmem((NJ, NY - 1, NX, RW, tail), BF16),
        vmem((NJ, NX, RW, tail), F32), vmem((NJ, NX, RW, tail), BF16),
        vmem((NJ, RW, tail), BF16), vmem((NJ, RW, tail), BF16),
        vmem((NJ, RW, tail), BF16), vmem((NJ, RW, tail), BF16),
        dma((3,)), dma((NJ, 5)), dma((NJ, 5)),
        dma((NJ, nu, 6)), dma((NJ, nu, 6)), dma((NJ, nu)), dma((NJ, nu)), dma((NJ,)), dma((NJ,)),
        dma((NJ, 6)), dma((NJ, 6)),
    ]
    return pl.pallas_call(
        kernel,
        out_shape=jax.ShapeDtypeStruct((NJ * RW, width), BF16),
        in_specs=[any_space, any_space, any_space, pl.BlockSpec(memory_space=pltpu.SMEM)],
        out_specs=pl.BlockSpec(memory_space=pltpu.VMEM),
        scratch_shapes=scratch,
        compiler_params=pltpu.CompilerParams(
            collective_id=0, has_side_effects=True, vmem_limit_bytes=56 * 1024 * 1024
        ),
        name="window",
    )(vt, screened, conduction_pairs, window_mask)


def solution(mesh):
    torus = Mesh(mesh.devices.reshape(2, NZ, 2, NY, NX), BAND + GA)
    return jax.shard_map(
        local,
        mesh=torus,
        in_specs=(P(None, BAND), P(BAND, GA), P(BAND, GA), P(None, BAND)),
        out_specs=P(GA, BAND),
        check_vma=False,
    )
```

```python
import jax
import jax.numpy as jnp
from jax import lax
from jax.experimental import pallas as pl
from jax.experimental.pallas import tpu as pltpu
from jax.sharding import Mesh
from jax.sharding import PartitionSpec as P

MESH = pl.DeviceIdType.MESH
BAND = ("yh", "z", "c")
GA = ("y", "x")
F32 = jnp.float32
BF16 = jnp.bfloat16

NZ, NY, NX = 8, 4, 4
NJ = 4
RW = 16
HOPS = (4, 3, 5, 2, 6, 1, 7)
UNITS = (
    ((0, 1024), (1024, 768)),
    ((0, 1024), (1024, 768)),
    ((0, 1024), (1024, 768)),
    ((0, 1024), (1024, 768)),
)
SPLIT = tuple(sum(units[-1]) for units in UNITS)
ORDER = (
    "S100", "S120", "S110", "S200", "S220", "S300", "S210", "S320", "S130", "S400", "PB00", "XF01",
    "XD01", "XF00", "S420", "S310", "XD00", "PB20", "XF20", "S230", "X200", "XD20", "XF21", "S410",
    "PB10", "X220", "X300", "XD21", "X201", "S330", "XF11", "XF10", "X221", "X320", "S430", "XD10",
    "XD11", "X301", "PB30", "XF30", "X211", "X321", "XF31", "X210", "XD30", "X230", "X311", "BS10",
    "XD31", "X310", "BS00", "X231", "BS20", "X330", "BS30", "YF11", "YF00", "X331", "B210", "B230",
    "B200", "YF21", "B220", "YF20", "B330", "YF01", "YF10", "B300", "B320", "YF30", "B310", "YF31",
)


def schedule():
    return [(step[:2], int(step[2]), int(step[3])) for step in ORDER]


def kernel(v_hbm, w_hbm, c_hbm, mask, out, v, w, cc, core_s, core_r, own, zs, zr, ysum, ys, yr,
           sv, pb, far_r, dir_r, mrg_s, mrg_r, ya_s, ya_r, yb_r, rb, rb16, bfar, bdir, bms, bmr,
           in_sem, one_s, one_r, xa_s, xa_r, ya_ss, ya_rs, yb_ss, yb_rs, xb_s, xb_r):
    yh, z, c = lax.axis_index("yh"), lax.axis_index("z"), lax.axis_index("c")
    y, x = lax.axis_index("y"), lax.axis_index("x")
    xp, xf, xm = lax.rem(x + 1, NX), lax.rem(x + 2, NX), lax.rem(x + 3, NX)

    loads = [
        pltpu.make_async_copy(v_hbm, v, in_sem.at[0]),
        pltpu.make_async_copy(w_hbm, w, in_sem.at[1]),
        pltpu.make_async_copy(c_hbm, cc, in_sem.at[2]),
    ]
    loads[0].start()
    loads[1].start()

    def at_z(k):
        return (yh, lax.rem(z + k, NZ), c, y, x)

    def at_y(k):
        return (yh, z, c, lax.rem(y + k, NY), x)

    partner = (yh, z, 1 - c, y, x)
    far = (1 - yh, z, c, y, x)
    right, left = (yh, z, c, y, xp), (yh, z, c, y, xm)

    barrier = pltpu.get_barrier_semaphore()
    peers = [at_z(k) for k in HOPS] + [far] + [at_y(k) for k in (1, 2, 3)] + [right, left, partner]
    for device in peers:
        pl.semaphore_signal(barrier, inc=1, device_id=device, device_id_type=MESH)

    def send(src, dst, s_sem, r_sem, device):
        pltpu.make_async_remote_copy(
            src_ref=src, dst_ref=dst, send_sem=s_sem, recv_sem=r_sem,
            device_id=device, device_id_type=MESH,
        ).start()

    def arrived(ref, sem):
        pltpu.make_async_copy(ref, ref, sem).wait()

    def partial(half, t):
        lanes = pl.ds(pl.multiple_of(half * 512 + t * 128, 128), 128)
        value = lax.dot_general(
            v[:, lanes], w[...], (((0,), (0,)), ((), ())), preferred_element_type=F32
        )
        return value.reshape(2, NJ, RW, -1)

    loads[0].wait()
    loads[1].wait()
    loads[2].start()

    def for_partner(t, carry):
        value = partial(1 - c, t).astype(BF16)
        for j in range(NJ):
            core_s[j, pl.ds(2 * t, 2)] = value[:, j]
        return carry

    lax.fori_loop(0, 4, for_partner, 0)
    pl.semaphore_wait(barrier, len(peers))
    for j in range(NJ):
        send(core_s.at[j], core_r.at[j], one_s.at[j, 0], one_r.at[j, 0], partner)

    def for_self(t, carry):
        value = partial(c, t)
        for j in range(NJ):
            own[j, pl.ds(2 * t, 2)] = value[:, j]
        return carry

    lax.fori_loop(0, 4, for_self, 0)

    def S1(j, u):
        arrived(core_r.at[j], one_r.at[j, 0])
        total = own[j] + core_r[j].astype(F32)
        own[j] = total
        zs[j] = total.astype(BF16)
        for k in HOPS:
            send(zs.at[j, lax.rem(z + k, NZ)], zr.at[j, k - 1],
                 one_s.at[j, 1], one_r.at[j, 1], at_z(k))

    def S2(j, u):
        arrived(zr.at[j], one_r.at[j, 1])
        total = own[j, z]
        for k in range(NZ - 1):
            total = total + zr[j, k].astype(F32)
        ysum[j] = total
        ys[j] = total.astype(BF16)
        send(ys.at[j], yr.at[j], one_s.at[j, 2], one_r.at[j, 2], far)

    def S3(j, u):
        arrived(yr.at[j], one_r.at[j, 2])
        mine = c * NZ + z
        sv[j, mine] = (ysum[j] + yr[j].astype(F32)).astype(BF16)
        for k in HOPS:
            send(sv.at[j, mine], sv.at[j, mine], one_s.at[j, 3], one_r.at[j, 3], at_z(k))

    def S4(j, u):
        arrived(zr.at[j], one_r.at[j, 3])
        half = sv.at[j, pl.ds(c * NZ, NZ)]
        send(half, half, one_s.at[j, 4], one_r.at[j, 4], partner)

    def product(j, first, count):
        rows = sv[j].reshape(256, -1)

        def tile(t, carry):
            at = pl.multiple_of(first + t * 256, 256)
            block = lax.dot_general(
                rows, cc[pl.ds(at, 256), :], (((1,), (1,)), ((), ())), preferred_element_type=F32
            )
            pb[j, :, :, :, pl.ds(at, 256)] = block.astype(BF16).reshape(NY, NX, RW, 256)
            return carry

        lax.fori_loop(0, count // 256, tile, 0)

    width = out.shape[1]

    def tail(j):
        return width - SPLIT[j]

    def b_cols(j):
        return pl.ds(SPLIT[j], tail(j))

    def yb_in(j):
        return yb_r.at[j, :, :, :, pl.ds(0, tail(j))]

    def PB(j, u):
        arrived(sv.at[j, pl.ds(0, NZ)], one_r.at[j, 4])
        if j == 0:
            loads[2].wait()
        product(j, SPLIT[j], tail(j))
        for k in (3, 2, 1):
            send(pb.at[j, lax.rem(y + k, NY), :, :, b_cols(j)], yb_in(j).at[k - 1],
                 yb_ss.at[j], yb_rs.at[j], at_y(k))

    def halves(j, u):
        lo, w_u = UNITS[j][u]
        return pl.ds(lo, w_u // 2), pl.ds(lo + w_u // 2, w_u // 2)

    def XF(j, u):
        product(j, *UNITS[j][u])
        h0, h1 = halves(j, u)
        send(pb.at[j, :, xf, :, h0], far_r.at[j, :, :, h0], xa_s.at[j, u, 0], xa_r.at[j, u, 0], right)
        send(pb.at[j, :, xf, :, h1], far_r.at[j, :, :, h1], xa_s.at[j, u, 1], xa_r.at[j, u, 1], left)

    def XD(j, u):
        h0, h1 = halves(j, u)
        send(pb.at[j, :, xp, :, h1], dir_r.at[j, :, :, h1], xa_s.at[j, u, 2], xa_r.at[j, u, 2], right)
        send(pb.at[j, :, xm, :, h0], dir_r.at[j, :, :, h0], xa_s.at[j, u, 3], xa_r.at[j, u, 3], left)

    def X2(j, u):
        for i, (h, to, device) in enumerate(zip(halves(j, u), (xp, xm), (right, left))):
            arrived(far_r.at[j, :, :, h], xa_r.at[j, u, i])
            mrg_s[j, :, :, h] = (pb[j, :, to, :, h].astype(F32) + far_r[j, :, :, h].astype(F32)).astype(BF16)
            send(mrg_s.at[j, :, :, h], mrg_r.at[j, :, :, h], xa_s.at[j, u, 4 + i], xa_r.at[j, u, 4 + i], device)

    def X3(j, u):
        h0, h1 = halves(j, u)
        arrived(dir_r.at[j, :, :, h1], xa_r.at[j, u, 2])
        arrived(dir_r.at[j, :, :, h0], xa_r.at[j, u, 3])
        arrived(mrg_r.at[j, :, :, h0], xa_r.at[j, u, 4])
        arrived(mrg_r.at[j, :, :, h1], xa_r.at[j, u, 5])
        cols = pl.ds(*UNITS[j][u])
        for k in (3, 2, 1):
            yd = lax.rem(y + k, NY)
            ya_s[j, k - 1, :, cols] = (
                pb[j, yd, x, :, cols].astype(F32) + dir_r[j, yd, :, cols].astype(F32)
                + mrg_r[j, yd, :, cols].astype(F32)
            ).astype(BF16)
            send(ya_s.at[j, k - 1, :, cols], ya_r.at[j, k - 1, :, cols],
                 ya_ss.at[j, u], ya_rs.at[j, u], at_y(k))

    row_block = (y * NX + x) // 2

    def finish(j, first, value):
        for t in range(value.shape[1] // 128):
            live = mask[row_block, first // 128 + t].astype(F32)
            out[j * RW:(j + 1) * RW, first + t * 128:first + (t + 1) * 128] = (
                value[:, t * 128:(t + 1) * 128] * live
            ).astype(BF16)

    def YF(j, u):
        lo, w_u = UNITS[j][u]
        cols = pl.ds(lo, w_u)
        arrived(ya_r.at[j, :, :, cols], ya_rs.at[j, u])
        total = (
            pb[j, y, x, :, cols].astype(F32) + dir_r[j, y, :, cols].astype(F32)
            + mrg_r[j, y, :, cols].astype(F32)
        )
        for k in range(3):
            total = total + ya_r[j, k, :, cols].astype(F32)
        finish(j, lo, total)

    def b_halves(j):
        return pl.ds(0, tail(j) // 2), pl.ds(tail(j) // 2, tail(j) // 2)

    def BS(j, u):
        arrived(yb_in(j), yb_rs.at[j])
        cols = pl.ds(0, tail(j))
        total = pb[j, y, :, :, b_cols(j)].astype(F32)
        for k in range(3):
            total = total + yb_r[j, k, :, :, cols].astype(F32)
        rb[j, :, :, cols] = total
        rb16[j, :, :, cols] = total.astype(BF16)
        b0, b1 = b_halves(j)
        send(rb16.at[j, xf, :, b0], bfar.at[j, :, b0], xb_s.at[j, 0], xb_r.at[j, 0], right)
        send(rb16.at[j, xf, :, b1], bfar.at[j, :, b1], xb_s.at[j, 1], xb_r.at[j, 1], left)
        send(rb16.at[j, xp, :, b1], bdir.at[j, :, b1], xb_s.at[j, 2], xb_r.at[j, 2], right)
        send(rb16.at[j, xm, :, b0], bdir.at[j, :, b0], xb_s.at[j, 3], xb_r.at[j, 3], left)

    def B2(j, u):
        for i, (h, to, device) in enumerate(zip(b_halves(j), (xp, xm), (right, left))):
            arrived(bfar.at[j, :, h], xb_r.at[j, i])
            bms[j, :, h] = (rb[j, to, :, h] + bfar[j, :, h].astype(F32)).astype(BF16)
            send(bms.at[j, :, h], bmr.at[j, :, h], xb_s.at[j, 4 + i], xb_r.at[j, 4 + i], device)

    def B3(j, u):
        b0, b1 = b_halves(j)
        arrived(bdir.at[j, :, b1], xb_r.at[j, 2])
        arrived(bdir.at[j, :, b0], xb_r.at[j, 3])
        arrived(bmr.at[j, :, b0], xb_r.at[j, 4])
        arrived(bmr.at[j, :, b1], xb_r.at[j, 5])
        cols = pl.ds(0, tail(j))
        finish(j, SPLIT[j], rb[j, x, :, cols] + bdir[j, :, cols].astype(F32) + bmr[j, :, cols].astype(F32))

    steps = dict(S1=S1, S2=S2, S3=S3, S4=S4, PB=PB, XF=XF, XD=XD, X2=X2, X3=X3, YF=YF, BS=BS, B2=B2, B3=B3)
    for name, j, u in schedule():
        steps[name](j, u)

    for j in range(NJ):
        arrived(core_s.at[j], one_s.at[j, 0])
        arrived(zr.at[j], one_s.at[j, 1])
        arrived(ys.at[j], one_s.at[j, 2])
        arrived(zr.at[j], one_s.at[j, 3])
        arrived(sv.at[j, pl.ds(0, NZ)], one_s.at[j, 4])
        for u, (lo, w_u) in enumerate(UNITS[j]):
            for slot in range(6):
                arrived(far_r.at[j, :, :, pl.ds(lo, w_u // 2)], xa_s.at[j, u, slot])
            arrived(ya_r.at[j, :, :, pl.ds(lo, w_u)], ya_ss.at[j, u])
        arrived(yb_in(j), yb_ss.at[j])
        for slot in range(6):
            arrived(bfar.at[j, :, b_halves(j)[0]], xb_s.at[j, slot])


def local(valence_pairs, screened, conduction_pairs, window_mask):
    inner = screened.shape[1]
    width = conduction_pairs.shape[0]
    head, tail = max(SPLIT), width - min(SPLIT)
    vt = valence_pairs.T
    vmem, dma = pltpu.VMEM, pltpu.SemaphoreType.DMA
    any_space = pl.BlockSpec(memory_space=pltpu.HBM)
    nu = max(len(units) for units in UNITS)
    scratch = [
        vmem(vt.shape, BF16), vmem(screened.shape, BF16), vmem(conduction_pairs.shape, BF16),
        vmem((NJ, NZ, RW, inner), BF16), vmem((NJ, NZ, RW, inner), BF16),
        vmem((NJ, NZ, RW, inner), F32),
        vmem((NJ, NZ, RW, inner), BF16), vmem((NJ, NZ - 1, RW, inner), BF16),
        vmem((NJ, RW, inner), F32), vmem((NJ, RW, inner), BF16), vmem((NJ, RW, inner), BF16),
        vmem((NJ, 2 * NZ, RW, inner), BF16),
        vmem((NJ, NY, NX, RW, width), BF16),
        vmem((NJ, NY, RW, head), BF16), vmem((NJ, NY, RW, head), BF16),
        vmem((NJ, NY, RW, head), BF16), vmem((NJ, NY, RW, head), BF16),
        vmem((NJ, NY - 1, RW, head), BF16), vmem((NJ, NY - 1, RW, head), BF16),
        vmem((NJ, NY - 1, NX, RW, tail), BF16),
        vmem((NJ, NX, RW, tail), F32), vmem((NJ, NX, RW, tail), BF16),
        vmem((NJ, RW, tail), BF16), vmem((NJ, RW, tail), BF16),
        vmem((NJ, RW, tail), BF16), vmem((NJ, RW, tail), BF16),
        dma((3,)), dma((NJ, 5)), dma((NJ, 5)),
        dma((NJ, nu, 6)), dma((NJ, nu, 6)), dma((NJ, nu)), dma((NJ, nu)), dma((NJ,)), dma((NJ,)),
        dma((NJ, 6)), dma((NJ, 6)),
    ]
    return pl.pallas_call(
        kernel,
        out_shape=jax.ShapeDtypeStruct((NJ * RW, width), BF16),
        in_specs=[any_space, any_space, any_space, pl.BlockSpec(memory_space=pltpu.SMEM)],
        out_specs=pl.BlockSpec(memory_space=pltpu.VMEM),
        scratch_shapes=scratch,
        compiler_params=pltpu.CompilerParams(
            collective_id=0, has_side_effects=True, vmem_limit_bytes=56 * 1024 * 1024
        ),
        name="window",
    )(vt, screened, conduction_pairs, window_mask)


def solution(mesh):
    torus = Mesh(mesh.devices.reshape(2, NZ, 2, NY, NX), BAND + GA)
    return jax.shard_map(
        local,
        mesh=torus,
        in_specs=(P(None, BAND), P(BAND, GA), P(BAND, GA), P(None, BAND)),
        out_specs=P(GA, BAND),
        check_vma=False,
    )
```

```python
import jax
import jax.numpy as jnp
from jax import lax
from jax.experimental import pallas as pl
from jax.experimental.pallas import tpu as pltpu
from jax.sharding import Mesh
from jax.sharding import PartitionSpec as P

MESH = pl.DeviceIdType.MESH
BAND = ("yh", "z", "c")
GA = ("y", "x")
F32 = jnp.float32
BF16 = jnp.bfloat16

NZ, NY, NX = 8, 4, 4
NJ = 4
RW = 16
HOPS = (4, 3, 5, 2, 6, 1, 7)
UNITS = (
    ((0, 1024), (1024, 768)),
    ((0, 1024), (1024, 768)),
    ((0, 1024), (1024, 768)),
    ((0, 1024), (1024, 768)),
)
SPLIT = tuple(sum(units[-1]) for units in UNITS)
ORDER = (
    "S100", "S120", "S110", "S200", "S220", "S300", "S210", "S320", "S130", "S400", "PB00", "XF01",
    "XD01", "XF00", "S420", "S310", "XD00", "PB20", "XF20", "S230", "X200", "XD20", "XF21", "S410",
    "PB10", "X220", "X300", "XD21", "X201", "S330", "XF11", "XF10", "X221", "X320", "S430", "XD10",
    "XD11", "X301", "PB30", "XF30", "X211", "X321", "XF31", "X210", "XD30", "X230", "X311", "BS10",
    "XD31", "X310", "BS00", "X231", "BS20", "X330", "BS30", "YF11", "YF00", "X331", "B210", "B230",
    "B200", "YF21", "B220", "YF20", "B330", "YF01", "YF10", "B300", "B320", "YF30", "B310", "YF31",
)


def schedule():
    return [(step[:2], int(step[2]), int(step[3])) for step in ORDER]


def kernel(v_hbm, w_hbm, c_hbm, mask, out, v, w, cc, core_s, core_r, own, zs, zr, ysum, ys, yr,
           sv, pb, far_r, dir_r, mrg_s, mrg_r, ya_s, ya_r, yb_r, rb, rb16, bfar, bdir, bms, bmr,
           in_sem, one_s, one_r, xa_s, xa_r, ya_ss, ya_rs, yb_ss, yb_rs, xb_s, xb_r):
    yh, z, c = lax.axis_index("yh"), lax.axis_index("z"), lax.axis_index("c")
    y, x = lax.axis_index("y"), lax.axis_index("x")
    xp, xf, xm = lax.rem(x + 1, NX), lax.rem(x + 2, NX), lax.rem(x + 3, NX)

    loads = [
        pltpu.make_async_copy(v_hbm, v, in_sem.at[0]),
        pltpu.make_async_copy(w_hbm, w, in_sem.at[1]),
        pltpu.make_async_copy(c_hbm, cc, in_sem.at[2]),
    ]
    loads[0].start()
    loads[1].start()

    def at_z(k):
        return (yh, lax.rem(z + k, NZ), c, y, x)

    def at_y(k):
        return (yh, z, c, lax.rem(y + k, NY), x)

    partner = (yh, z, 1 - c, y, x)
    far = (1 - yh, z, c, y, x)
    right, left = (yh, z, c, y, xp), (yh, z, c, y, xm)

    barrier = pltpu.get_barrier_semaphore()
    peers = [at_z(k) for k in HOPS] + [far] + [at_y(k) for k in (1, 2, 3)] + [right, left, partner]
    for device in peers:
        pl.semaphore_signal(barrier, inc=1, device_id=device, device_id_type=MESH)

    def send(src, dst, s_sem, r_sem, device):
        pltpu.make_async_remote_copy(
            src_ref=src, dst_ref=dst, send_sem=s_sem, recv_sem=r_sem,
            device_id=device, device_id_type=MESH,
        ).start()

    def arrived(ref, sem):
        pltpu.make_async_copy(ref, ref, sem).wait()

    def partial(half, t):
        lanes = pl.ds(pl.multiple_of(half * 512 + t * 128, 128), 128)
        value = lax.dot_general(
            v[:, lanes], w[...], (((0,), (0,)), ((), ())), preferred_element_type=F32
        )
        return value.reshape(2, NJ, RW, -1)

    loads[0].wait()
    loads[1].wait()
    loads[2].start()

    def for_partner(t, carry):
        value = partial(1 - c, t).astype(BF16)
        for j in range(NJ):
            core_s[j, pl.ds(2 * t, 2)] = value[:, j]
        return carry

    lax.fori_loop(0, 4, for_partner, 0)
    pl.semaphore_wait(barrier, len(peers))
    for j in range(NJ):
        send(core_s.at[j], core_r.at[j], one_s.at[j, 0], one_r.at[j, 0], partner)

    def for_self(t, carry):
        value = partial(c, t)
        for j in range(NJ):
            own[j, pl.ds(2 * t, 2)] = value[:, j]
        return carry

    lax.fori_loop(0, 4, for_self, 0)

    def S1(j, u):
        arrived(core_r.at[j], one_r.at[j, 0])

        def add(i, carry):
            total = own[j, i] + core_r[j, i].astype(F32)
            own[j, i] = total
            zs[j, i] = total.astype(BF16)
            return carry

        lax.fori_loop(0, NZ, add, 0)
        for k in HOPS:
            send(zs.at[j, lax.rem(z + k, NZ)], zr.at[j, k - 1],
                 one_s.at[j, 1], one_r.at[j, 1], at_z(k))

    def S2(j, u):
        arrived(zr.at[j], one_r.at[j, 1])
        total = own[j, z]
        for k in range(NZ - 1):
            total = total + zr[j, k].astype(F32)
        ysum[j] = total
        ys[j] = total.astype(BF16)
        send(ys.at[j], yr.at[j], one_s.at[j, 2], one_r.at[j, 2], far)

    def S3(j, u):
        arrived(yr.at[j], one_r.at[j, 2])
        mine = c * NZ + z
        sv[j, mine] = (ysum[j] + yr[j].astype(F32)).astype(BF16)
        for k in HOPS:
            send(sv.at[j, mine], sv.at[j, mine], one_s.at[j, 3], one_r.at[j, 3], at_z(k))

    def S4(j, u):
        arrived(zr.at[j], one_r.at[j, 3])
        half = sv.at[j, pl.ds(c * NZ, NZ)]
        send(half, half, one_s.at[j, 4], one_r.at[j, 4], partner)

    def product(j, first, count):
        rows = sv[j].reshape(256, -1)

        def tile(t, carry):
            at = pl.multiple_of(first + t * 256, 256)
            block = lax.dot_general(
                rows, cc[pl.ds(at, 256), :], (((1,), (1,)), ((), ())), preferred_element_type=F32
            )
            pb[j, :, :, :, pl.ds(at, 256)] = block.astype(BF16).reshape(NY, NX, RW, 256)
            return carry

        lax.fori_loop(0, count // 256, tile, 0)

    width = out.shape[1]

    def tail(j):
        return width - SPLIT[j]

    def b_cols(j):
        return pl.ds(SPLIT[j], tail(j))

    def yb_in(j):
        return yb_r.at[j, :, :, :, pl.ds(0, tail(j))]

    def PB(j, u):
        arrived(sv.at[j, pl.ds(0, NZ)], one_r.at[j, 4])
        if j == 0:
            loads[2].wait()
        product(j, SPLIT[j], tail(j))
        for k in (3, 2, 1):
            send(pb.at[j, lax.rem(y + k, NY), :, :, b_cols(j)], yb_in(j).at[k - 1],
                 yb_ss.at[j], yb_rs.at[j], at_y(k))

    def halves(j, u):
        lo, w_u = UNITS[j][u]
        return pl.ds(lo, w_u // 2), pl.ds(lo + w_u // 2, w_u // 2)

    def XF(j, u):
        product(j, *UNITS[j][u])
        h0, h1 = halves(j, u)
        send(pb.at[j, :, xf, :, h0], far_r.at[j, :, :, h0], xa_s.at[j, u, 0], xa_r.at[j, u, 0], right)
        send(pb.at[j, :, xf, :, h1], far_r.at[j, :, :, h1], xa_s.at[j, u, 1], xa_r.at[j, u, 1], left)

    def XD(j, u):
        h0, h1 = halves(j, u)
        send(pb.at[j, :, xp, :, h1], dir_r.at[j, :, :, h1], xa_s.at[j, u, 2], xa_r.at[j, u, 2], right)
        send(pb.at[j, :, xm, :, h0], dir_r.at[j, :, :, h0], xa_s.at[j, u, 3], xa_r.at[j, u, 3], left)

    def X2(j, u):
        for i, (h, to, device) in enumerate(zip(halves(j, u), (xp, xm), (right, left))):
            arrived(far_r.at[j, :, :, h], xa_r.at[j, u, i])

            def add(i, carry):
                mrg_s[j, i, :, h] = (
                    pb[j, i, to, :, h].astype(F32) + far_r[j, i, :, h].astype(F32)
                ).astype(BF16)
                return carry

            lax.fori_loop(0, NY, add, 0)
            send(mrg_s.at[j, :, :, h], mrg_r.at[j, :, :, h], xa_s.at[j, u, 4 + i], xa_r.at[j, u, 4 + i], device)

    def X3(j, u):
        h0, h1 = halves(j, u)
        arrived(dir_r.at[j, :, :, h1], xa_r.at[j, u, 2])
        arrived(dir_r.at[j, :, :, h0], xa_r.at[j, u, 3])
        arrived(mrg_r.at[j, :, :, h0], xa_r.at[j, u, 4])
        arrived(mrg_r.at[j, :, :, h1], xa_r.at[j, u, 5])
        cols = pl.ds(*UNITS[j][u])

        def add(i, carry):
            yd = lax.rem(y + 1 + i, NY)
            ya_s[j, i, :, cols] = (
                pb[j, yd, x, :, cols].astype(F32) + dir_r[j, yd, :, cols].astype(F32)
                + mrg_r[j, yd, :, cols].astype(F32)
            ).astype(BF16)
            return carry

        lax.fori_loop(0, NY - 1, add, 0)
        for k in (3, 2, 1):
            send(ya_s.at[j, k - 1, :, cols], ya_r.at[j, k - 1, :, cols],
                 ya_ss.at[j, u], ya_rs.at[j, u], at_y(k))

    row_block = (y * NX + x) // 2

    def finish(j, first, value):
        for t in range(value.shape[1] // 128):
            live = mask[row_block, first // 128 + t].astype(F32)
            out[j * RW:(j + 1) * RW, first + t * 128:first + (t + 1) * 128] = (
                value[:, t * 128:(t + 1) * 128] * live
            ).astype(BF16)

    def YF(j, u):
        lo, w_u = UNITS[j][u]
        cols = pl.ds(lo, w_u)
        arrived(ya_r.at[j, :, :, cols], ya_rs.at[j, u])

        def add(i, carry):
            at = pl.multiple_of(lo + i * 256, 256)
            cols = pl.ds(at, 256)
            total = (
                pb[j, y, x, :, cols].astype(F32) + dir_r[j, y, :, cols].astype(F32)
                + mrg_r[j, y, :, cols].astype(F32)
            )
            for k in range(3):
                total = total + ya_r[j, k, :, cols].astype(F32)
            for t in range(2):
                live = mask[row_block, lo // 128 + 2 * i + t].astype(F32)
                out[j * RW:(j + 1) * RW, pl.ds(pl.multiple_of(at + t * 128, 128), 128)] = (
                    total[:, t * 128:(t + 1) * 128] * live
                ).astype(BF16)
            return carry

        lax.fori_loop(0, w_u // 256, add, 0)

    def b_halves(j):
        return pl.ds(0, tail(j) // 2), pl.ds(tail(j) // 2, tail(j) // 2)

    def BS(j, u):
        arrived(yb_in(j), yb_rs.at[j])
        cols = pl.ds(0, tail(j))

        def add(i, carry):
            total = pb[j, y, i, :, b_cols(j)].astype(F32)
            for k in range(3):
                total = total + yb_r[j, k, i, :, cols].astype(F32)
            rb[j, i, :, cols] = total
            rb16[j, i, :, cols] = total.astype(BF16)
            return carry

        lax.fori_loop(0, NX, add, 0)
        b0, b1 = b_halves(j)
        send(rb16.at[j, xf, :, b0], bfar.at[j, :, b0], xb_s.at[j, 0], xb_r.at[j, 0], right)
        send(rb16.at[j, xf, :, b1], bfar.at[j, :, b1], xb_s.at[j, 1], xb_r.at[j, 1], left)
        send(rb16.at[j, xp, :, b1], bdir.at[j, :, b1], xb_s.at[j, 2], xb_r.at[j, 2], right)
        send(rb16.at[j, xm, :, b0], bdir.at[j, :, b0], xb_s.at[j, 3], xb_r.at[j, 3], left)

    def B2(j, u):
        for i, (h, to, device) in enumerate(zip(b_halves(j), (xp, xm), (right, left))):
            arrived(bfar.at[j, :, h], xb_r.at[j, i])
            bms[j, :, h] = (rb[j, to, :, h] + bfar[j, :, h].astype(F32)).astype(BF16)
            send(bms.at[j, :, h], bmr.at[j, :, h], xb_s.at[j, 4 + i], xb_r.at[j, 4 + i], device)

    def B3(j, u):
        b0, b1 = b_halves(j)
        arrived(bdir.at[j, :, b1], xb_r.at[j, 2])
        arrived(bdir.at[j, :, b0], xb_r.at[j, 3])
        arrived(bmr.at[j, :, b0], xb_r.at[j, 4])
        arrived(bmr.at[j, :, b1], xb_r.at[j, 5])
        cols = pl.ds(0, tail(j))
        finish(j, SPLIT[j], rb[j, x, :, cols] + bdir[j, :, cols].astype(F32) + bmr[j, :, cols].astype(F32))

    steps = dict(S1=S1, S2=S2, S3=S3, S4=S4, PB=PB, XF=XF, XD=XD, X2=X2, X3=X3, YF=YF, BS=BS, B2=B2, B3=B3)
    for name, j, u in schedule():
        steps[name](j, u)

    for j in range(NJ):
        arrived(core_s.at[j], one_s.at[j, 0])
        arrived(zr.at[j], one_s.at[j, 1])
        arrived(ys.at[j], one_s.at[j, 2])
        arrived(zr.at[j], one_s.at[j, 3])
        arrived(sv.at[j, pl.ds(0, NZ)], one_s.at[j, 4])
        for u, (lo, w_u) in enumerate(UNITS[j]):
            for slot in range(6):
                arrived(far_r.at[j, :, :, pl.ds(lo, w_u // 2)], xa_s.at[j, u, slot])
            arrived(ya_r.at[j, :, :, pl.ds(lo, w_u)], ya_ss.at[j, u])
        arrived(yb_in(j), yb_ss.at[j])
        for slot in range(6):
            arrived(bfar.at[j, :, b_halves(j)[0]], xb_s.at[j, slot])


def local(valence_pairs, screened, conduction_pairs, window_mask):
    inner = screened.shape[1]
    width = conduction_pairs.shape[0]
    head, tail = max(SPLIT), width - min(SPLIT)
    vt = valence_pairs.T
    vmem, dma = pltpu.VMEM, pltpu.SemaphoreType.DMA
    any_space = pl.BlockSpec(memory_space=pltpu.HBM)
    nu = max(len(units) for units in UNITS)
    scratch = [
        vmem(vt.shape, BF16), vmem(screened.shape, BF16), vmem(conduction_pairs.shape, BF16),
        vmem((NJ, NZ, RW, inner), BF16), vmem((NJ, NZ, RW, inner), BF16),
        vmem((NJ, NZ, RW, inner), F32),
        vmem((NJ, NZ, RW, inner), BF16), vmem((NJ, NZ - 1, RW, inner), BF16),
        vmem((NJ, RW, inner), F32), vmem((NJ, RW, inner), BF16), vmem((NJ, RW, inner), BF16),
        vmem((NJ, 2 * NZ, RW, inner), BF16),
        vmem((NJ, NY, NX, RW, width), BF16),
        vmem((NJ, NY, RW, head), BF16), vmem((NJ, NY, RW, head), BF16),
        vmem((NJ, NY, RW, head), BF16), vmem((NJ, NY, RW, head), BF16),
        vmem((NJ, NY - 1, RW, head), BF16), vmem((NJ, NY - 1, RW, head), BF16),
        vmem((NJ, NY - 1, NX, RW, tail), BF16),
        vmem((NJ, NX, RW, tail), F32), vmem((NJ, NX, RW, tail), BF16),
        vmem((NJ, RW, tail), BF16), vmem((NJ, RW, tail), BF16),
        vmem((NJ, RW, tail), BF16), vmem((NJ, RW, tail), BF16),
        dma((3,)), dma((NJ, 5)), dma((NJ, 5)),
        dma((NJ, nu, 6)), dma((NJ, nu, 6)), dma((NJ, nu)), dma((NJ, nu)), dma((NJ,)), dma((NJ,)),
        dma((NJ, 6)), dma((NJ, 6)),
    ]
    return pl.pallas_call(
        kernel,
        out_shape=jax.ShapeDtypeStruct((NJ * RW, width), BF16),
        in_specs=[any_space, any_space, any_space, pl.BlockSpec(memory_space=pltpu.SMEM)],
        out_specs=pl.BlockSpec(memory_space=pltpu.VMEM),
        scratch_shapes=scratch,
        compiler_params=pltpu.CompilerParams(
            collective_id=0, has_side_effects=True, vmem_limit_bytes=56200000
        ),
        name="window",
    )(vt, screened, conduction_pairs, window_mask)


def solution(mesh):
    torus = Mesh(mesh.devices.reshape(2, NZ, 2, NY, NX), BAND + GA)
    return jax.shard_map(
        local,
        mesh=torus,
        in_specs=(P(None, BAND), P(BAND, GA), P(BAND, GA), P(None, BAND)),
        out_specs=P(GA, BAND),
        check_vma=False,
    )
```

```python
import jax
import jax.numpy as jnp
from jax import lax
from jax.experimental import pallas as pl
from jax.experimental.pallas import tpu as pltpu
from jax.sharding import Mesh
from jax.sharding import PartitionSpec as P

MESH = pl.DeviceIdType.MESH
BAND = ("yh", "z", "c")
GA = ("y", "x")
F32 = jnp.float32
BF16 = jnp.bfloat16

NZ, NY, NX = 8, 4, 4
NJ = 4
RW = 16
HOPS = (4, 3, 5, 2, 6, 1, 7)
UNITS = (
    ((0, 1024), (1024, 768)),
    ((0, 1024), (1024, 768)),
    ((0, 1024), (1024, 768)),
    ((0, 1024), (1024, 768)),
)
SPLIT = tuple(sum(units[-1]) for units in UNITS)
ORDER = (
    "S100", "S120", "S110", "S200", "S220", "S300", "S210", "S320", "S400", "S130", "PB00", "XF01",
    "XD01", "XF00", "S420", "S310", "XD00", "PB20", "XF20", "S230", "X200", "XD20", "XF21", "S410",
    "PB10", "X220", "X300", "XD21", "X201", "S330", "XF11", "XF10", "X221", "X320", "S430", "XD10",
    "XD11", "X301", "PB30", "XF30", "X211", "X321", "XF31", "X210", "XD30", "X230", "X311", "BS10",
    "XD31", "X310", "BS00", "X231", "BS20", "X330", "BS30", "YF11", "YF00", "X331", "B210", "B230",
    "B200", "YF21", "B220", "YF20", "B330", "YF01", "YF10", "B300", "B320", "YF30", "B310", "YF31",
)


def schedule():
    return [(step[:2], int(step[2]), int(step[3])) for step in ORDER]


def kernel(v_hbm, w_hbm, c_hbm, mask, out, v, w, cc, core_s, core_r, own, zs, zr, ysum, ys, yr,
           sv, pb, far_r, dir_r, mrg_s, mrg_r, ya_s, ya_r, yb_r, rb, rb16, bfar, bdir, bms, bmr,
           in_sem, one_s, one_r, xa_s, xa_r, ya_ss, ya_rs, yb_ss, yb_rs, xb_s, xb_r):
    yh, z, c = lax.axis_index("yh"), lax.axis_index("z"), lax.axis_index("c")
    y, x = lax.axis_index("y"), lax.axis_index("x")
    xp, xf, xm = lax.rem(x + 1, NX), lax.rem(x + 2, NX), lax.rem(x + 3, NX)

    loads = [
        pltpu.make_async_copy(v_hbm, v, in_sem.at[0]),
        pltpu.make_async_copy(w_hbm, w, in_sem.at[1]),
        pltpu.make_async_copy(c_hbm, cc, in_sem.at[2]),
    ]
    loads[0].start()
    loads[1].start()

    def at_z(k):
        return (yh, lax.rem(z + k, NZ), c, y, x)

    def at_y(k):
        return (yh, z, c, lax.rem(y + k, NY), x)

    partner = (yh, z, 1 - c, y, x)
    far = (1 - yh, z, c, y, x)
    right, left = (yh, z, c, y, xp), (yh, z, c, y, xm)

    barrier = pltpu.get_barrier_semaphore()
    peers = [at_z(k) for k in HOPS] + [far] + [at_y(k) for k in (1, 2, 3)] + [right, left, partner]
    for device in peers:
        pl.semaphore_signal(barrier, inc=1, device_id=device, device_id_type=MESH)

    def send(src, dst, s_sem, r_sem, device):
        pltpu.make_async_remote_copy(
            src_ref=src, dst_ref=dst, send_sem=s_sem, recv_sem=r_sem,
            device_id=device, device_id_type=MESH,
        ).start()

    def arrived(ref, sem):
        pltpu.make_async_copy(ref, ref, sem).wait()

    def partial(half, t):
        lanes = pl.ds(pl.multiple_of(half * 512 + t * 128, 128), 128)
        value = lax.dot_general(
            v[:, lanes], w[...], (((0,), (0,)), ((), ())), preferred_element_type=F32
        )
        return value.reshape(2, NJ, RW, -1)

    loads[0].wait()
    loads[1].wait()
    loads[2].start()

    def for_partner(t, carry):
        value = partial(1 - c, t).astype(BF16)
        for j in range(NJ):
            core_s[j, pl.ds(2 * t, 2)] = value[:, j]
        return carry

    lax.fori_loop(0, 4, for_partner, 0)
    pl.semaphore_wait(barrier, len(peers))
    for j in range(NJ):
        send(core_s.at[j], core_r.at[j], one_s.at[j, 0], one_r.at[j, 0], partner)

    def for_self(t, carry):
        value = partial(c, t)
        for j in range(NJ):
            own[j, pl.ds(2 * t, 2)] = value[:, j]
        return carry

    lax.fori_loop(0, 4, for_self, 0)

    def S1(j, u):
        arrived(core_r.at[j], one_r.at[j, 0])

        def add(i, carry):
            total = own[j, i] + core_r[j, i].astype(F32)
            own[j, i] = total
            zs[j, i] = total.astype(BF16)
            return carry

        lax.fori_loop(0, NZ, add, 0)
        for k in HOPS:
            send(zs.at[j, lax.rem(z + k, NZ)], zr.at[j, k - 1],
                 one_s.at[j, 1], one_r.at[j, 1], at_z(k))

    def S2(j, u):
        arrived(zr.at[j], one_r.at[j, 1])
        total = own[j, z]
        for k in range(NZ - 1):
            total = total + zr[j, k].astype(F32)
        ysum[j] = total
        ys[j] = total.astype(BF16)
        send(ys.at[j], yr.at[j], one_s.at[j, 2], one_r.at[j, 2], far)

    def S3(j, u):
        arrived(yr.at[j], one_r.at[j, 2])
        mine = c * NZ + z
        sv[j, mine] = (ysum[j] + yr[j].astype(F32)).astype(BF16)
        for k in HOPS:
            send(sv.at[j, mine], sv.at[j, mine], one_s.at[j, 3], one_r.at[j, 3], at_z(k))

    def S4(j, u):
        arrived(zr.at[j], one_r.at[j, 3])
        half = sv.at[j, pl.ds(c * NZ, NZ)]
        send(half, half, one_s.at[j, 4], one_r.at[j, 4], partner)

    def product(j, first, count):
        rows = sv[j].reshape(256, -1)

        def tile(t, carry):
            at = pl.multiple_of(first + t * 256, 256)
            block = lax.dot_general(
                rows, cc[pl.ds(at, 256), :], (((1,), (1,)), ((), ())), preferred_element_type=F32
            )
            pb[j, :, :, :, pl.ds(at, 256)] = block.astype(BF16).reshape(NY, NX, RW, 256)
            return carry

        lax.fori_loop(0, count // 256, tile, 0)

    width = out.shape[1]

    def tail(j):
        return width - SPLIT[j]

    def b_cols(j):
        return pl.ds(SPLIT[j], tail(j))

    def yb_in(j):
        return yb_r.at[j, :, :, :, pl.ds(0, tail(j))]

    def PB(j, u):
        arrived(sv.at[j, pl.ds(0, NZ)], one_r.at[j, 4])
        if j == 0:
            loads[2].wait()
        product(j, SPLIT[j], tail(j))
        for k in (3, 2, 1):
            send(pb.at[j, lax.rem(y + k, NY), :, :, b_cols(j)], yb_in(j).at[k - 1],
                 yb_ss.at[j], yb_rs.at[j], at_y(k))

    def halves(j, u):
        lo, w_u = UNITS[j][u]
        return pl.ds(lo, w_u // 2), pl.ds(lo + w_u // 2, w_u // 2)

    def XF(j, u):
        product(j, *UNITS[j][u])
        h0, h1 = halves(j, u)
        send(pb.at[j, :, xf, :, h0], far_r.at[j, :, :, h0], xa_s.at[j, u, 0], xa_r.at[j, u, 0], right)
        send(pb.at[j, :, xf, :, h1], far_r.at[j, :, :, h1], xa_s.at[j, u, 1], xa_r.at[j, u, 1], left)

    def XD(j, u):
        h0, h1 = halves(j, u)
        send(pb.at[j, :, xp, :, h1], dir_r.at[j, :, :, h1], xa_s.at[j, u, 2], xa_r.at[j, u, 2], right)
        send(pb.at[j, :, xm, :, h0], dir_r.at[j, :, :, h0], xa_s.at[j, u, 3], xa_r.at[j, u, 3], left)

    def X2(j, u):
        for i, (h, to, device) in enumerate(zip(halves(j, u), (xp, xm), (right, left))):
            arrived(far_r.at[j, :, :, h], xa_r.at[j, u, i])

            def add(i, carry):
                mrg_s[j, i, :, h] = (
                    pb[j, i, to, :, h].astype(F32) + far_r[j, i, :, h].astype(F32)
                ).astype(BF16)
                return carry

            lax.fori_loop(0, NY, add, 0)
            send(mrg_s.at[j, :, :, h], mrg_r.at[j, :, :, h], xa_s.at[j, u, 4 + i], xa_r.at[j, u, 4 + i], device)

    def X3(j, u):
        h0, h1 = halves(j, u)
        arrived(dir_r.at[j, :, :, h1], xa_r.at[j, u, 2])
        arrived(dir_r.at[j, :, :, h0], xa_r.at[j, u, 3])
        arrived(mrg_r.at[j, :, :, h0], xa_r.at[j, u, 4])
        arrived(mrg_r.at[j, :, :, h1], xa_r.at[j, u, 5])
        cols = pl.ds(*UNITS[j][u])

        def add(i, carry):
            yd = lax.rem(y + 1 + i, NY)
            ya_s[j, i, :, cols] = (
                pb[j, yd, x, :, cols].astype(F32) + dir_r[j, yd, :, cols].astype(F32)
                + mrg_r[j, yd, :, cols].astype(F32)
            ).astype(BF16)
            return carry

        lax.fori_loop(0, NY - 1, add, 0)
        for k in (3, 2, 1):
            send(ya_s.at[j, k - 1, :, cols], ya_r.at[j, k - 1, :, cols],
                 ya_ss.at[j, u], ya_rs.at[j, u], at_y(k))

    row_block = (y * NX + x) // 2

    def finish(j, first, value):
        for t in range(value.shape[1] // 128):
            live = mask[row_block, first // 128 + t].astype(F32)
            out[j * RW:(j + 1) * RW, first + t * 128:first + (t + 1) * 128] = (
                value[:, t * 128:(t + 1) * 128] * live
            ).astype(BF16)

    def YF(j, u):
        lo, w_u = UNITS[j][u]
        cols = pl.ds(lo, w_u)
        arrived(ya_r.at[j, :, :, cols], ya_rs.at[j, u])

        def add(i, carry):
            at = pl.multiple_of(lo + i * 256, 256)
            cols = pl.ds(at, 256)
            total = (
                pb[j, y, x, :, cols].astype(F32) + dir_r[j, y, :, cols].astype(F32)
                + mrg_r[j, y, :, cols].astype(F32)
            )
            for k in range(3):
                total = total + ya_r[j, k, :, cols].astype(F32)
            for t in range(2):
                live = mask[row_block, lo // 128 + 2 * i + t].astype(F32)
                out[j * RW:(j + 1) * RW, pl.ds(pl.multiple_of(at + t * 128, 128), 128)] = (
                    total[:, t * 128:(t + 1) * 128] * live
                ).astype(BF16)
            return carry

        lax.fori_loop(0, w_u // 256, add, 0)

    def b_halves(j):
        return pl.ds(0, tail(j) // 2), pl.ds(tail(j) // 2, tail(j) // 2)

    def BS(j, u):
        arrived(yb_in(j), yb_rs.at[j])
        cols = pl.ds(0, tail(j))

        def add(i, carry):
            total = pb[j, y, i, :, b_cols(j)].astype(F32)
            for k in range(3):
                total = total + yb_r[j, k, i, :, cols].astype(F32)
            rb[j, i, :, cols] = total
            rb16[j, i, :, cols] = total.astype(BF16)
            return carry

        lax.fori_loop(0, NX, add, 0)
        b0, b1 = b_halves(j)
        send(rb16.at[j, xf, :, b0], bfar.at[j, :, b0], xb_s.at[j, 0], xb_r.at[j, 0], right)
        send(rb16.at[j, xf, :, b1], bfar.at[j, :, b1], xb_s.at[j, 1], xb_r.at[j, 1], left)
        send(rb16.at[j, xp, :, b1], bdir.at[j, :, b1], xb_s.at[j, 2], xb_r.at[j, 2], right)
        send(rb16.at[j, xm, :, b0], bdir.at[j, :, b0], xb_s.at[j, 3], xb_r.at[j, 3], left)

    def B2(j, u):
        for i, (h, to, device) in enumerate(zip(b_halves(j), (xp, xm), (right, left))):
            arrived(bfar.at[j, :, h], xb_r.at[j, i])
            bms[j, :, h] = (rb[j, to, :, h] + bfar[j, :, h].astype(F32)).astype(BF16)
            send(bms.at[j, :, h], bmr.at[j, :, h], xb_s.at[j, 4 + i], xb_r.at[j, 4 + i], device)

    def B3(j, u):
        b0, b1 = b_halves(j)
        arrived(bdir.at[j, :, b1], xb_r.at[j, 2])
        arrived(bdir.at[j, :, b0], xb_r.at[j, 3])
        arrived(bmr.at[j, :, b0], xb_r.at[j, 4])
        arrived(bmr.at[j, :, b1], xb_r.at[j, 5])
        cols = pl.ds(0, tail(j))
        finish(j, SPLIT[j], rb[j, x, :, cols] + bdir[j, :, cols].astype(F32) + bmr[j, :, cols].astype(F32))

    steps = dict(S1=S1, S2=S2, S3=S3, S4=S4, PB=PB, XF=XF, XD=XD, X2=X2, X3=X3, YF=YF, BS=BS, B2=B2, B3=B3)
    for name, j, u in schedule():
        steps[name](j, u)

    for j in range(NJ):
        arrived(core_s.at[j], one_s.at[j, 0])
        arrived(zr.at[j], one_s.at[j, 1])
        arrived(ys.at[j], one_s.at[j, 2])
        arrived(zr.at[j], one_s.at[j, 3])
        arrived(sv.at[j, pl.ds(0, NZ)], one_s.at[j, 4])
        for u, (lo, w_u) in enumerate(UNITS[j]):
            for slot in range(6):
                arrived(far_r.at[j, :, :, pl.ds(lo, w_u // 2)], xa_s.at[j, u, slot])
            arrived(ya_r.at[j, :, :, pl.ds(lo, w_u)], ya_ss.at[j, u])
        arrived(yb_in(j), yb_ss.at[j])
        for slot in range(6):
            arrived(bfar.at[j, :, b_halves(j)[0]], xb_s.at[j, slot])


def local(valence_pairs, screened, conduction_pairs, window_mask):
    inner = screened.shape[1]
    width = conduction_pairs.shape[0]
    head, tail = max(SPLIT), width - min(SPLIT)
    vt = valence_pairs.T
    vmem, dma = pltpu.VMEM, pltpu.SemaphoreType.DMA
    any_space = pl.BlockSpec(memory_space=pltpu.HBM)
    nu = max(len(units) for units in UNITS)
    scratch = [
        vmem(vt.shape, BF16), vmem(screened.shape, BF16), vmem(conduction_pairs.shape, BF16),
        vmem((NJ, NZ, RW, inner), BF16), vmem((NJ, NZ, RW, inner), BF16),
        vmem((NJ, NZ, RW, inner), F32),
        vmem((NJ, NZ, RW, inner), BF16), vmem((NJ, NZ - 1, RW, inner), BF16),
        vmem((NJ, RW, inner), F32), vmem((NJ, RW, inner), BF16), vmem((NJ, RW, inner), BF16),
        vmem((NJ, 2 * NZ, RW, inner), BF16),
        vmem((NJ, NY, NX, RW, width), BF16),
        vmem((NJ, NY, RW, head), BF16), vmem((NJ, NY, RW, head), BF16),
        vmem((NJ, NY, RW, head), BF16), vmem((NJ, NY, RW, head), BF16),
        vmem((NJ, NY - 1, RW, head), BF16), vmem((NJ, NY - 1, RW, head), BF16),
        vmem((NJ, NY - 1, NX, RW, tail), BF16),
        vmem((NJ, NX, RW, tail), F32), vmem((NJ, NX, RW, tail), BF16),
        vmem((NJ, RW, tail), BF16), vmem((NJ, RW, tail), BF16),
        vmem((NJ, RW, tail), BF16), vmem((NJ, RW, tail), BF16),
        dma((3,)), dma((NJ, 5)), dma((NJ, 5)),
        dma((NJ, nu, 6)), dma((NJ, nu, 6)), dma((NJ, nu)), dma((NJ, nu)), dma((NJ,)), dma((NJ,)),
        dma((NJ, 6)), dma((NJ, 6)),
    ]
    return pl.pallas_call(
        kernel,
        out_shape=jax.ShapeDtypeStruct((NJ * RW, width), BF16),
        in_specs=[any_space, any_space, any_space, pl.BlockSpec(memory_space=pltpu.SMEM)],
        out_specs=pl.BlockSpec(memory_space=pltpu.VMEM),
        scratch_shapes=scratch,
        compiler_params=pltpu.CompilerParams(
            collective_id=0, has_side_effects=True, vmem_limit_bytes=56200000
        ),
        name="window",
    )(vt, screened, conduction_pairs, window_mask)


def solution(mesh):
    torus = Mesh(mesh.devices.reshape(2, NZ, 2, NY, NX), BAND + GA)
    return jax.shard_map(
        local,
        mesh=torus,
        in_specs=(P(None, BAND), P(BAND, GA), P(BAND, GA), P(None, BAND)),
        out_specs=P(GA, BAND),
        check_vma=False,
    )
```
